32 devices in a mesh: scan: 8 (over y, x, core), tile: 4 (over z).
Axes of the slice: x: 2, y: 2, z: 4, core: 2. Of those that a mesh axis runs over, the one named last changes fastest.
Arguments:
- object_field: float32 [2, 2048, 1024], P(None, 'scan', 'tile'), may hold values from -4.2 to 4.2
- probe_modes: float32 [8, 2, 256, 256], P('tile'), may hold values from -2.1 to 2.1
- amplitudes: bfloat16 [64, 256, 256], P('scan'), may hold values from 0.25 to 3
- positions: int32 [64, 2], P('scan'), may hold values from 0 to 1792, as said below
- counts: int32 [8], P('scan'), may hold values from 1 to 8, as said below
Outputs:
- new_object: float32 [2, 2048, 1024], P(None, 'scan', 'tile')
- probe_step: float32 [8, 2, 256, 256], P('tile')
The draws below stay inside these ranges and needn't reach their ends.
Inputs may be any that keep to these rules, and one draw needn't show every extreme that they name: `positions`: slot j's row offset lies in rows (j // 8) * 256 to (j // 8) * 256 + 255; every window lies inside the object: row offsets at most 1792, column offsets at most 768. `counts`: some scan index holds 8 live slots and some holds one.
All inputs are finite; a program needn't handle non-finite values.
Results may differ from the reference program's by a relative error of at most 0.003.
Values may be sent and summed in bfloat16 or wider, within the bound.
No kernel may reach another device: no remote copies, remote signals or barrier semaphores. Data moves between devices by JAX's collectives and lax.ppermute only.
A program may use at most 128 MiB of HBM per device.

```python
import math
import jax
import jax.numpy as jnp
from jax import lax

W = 256
MODES = 8
SLOTS = 8
TR = 256
NOR = 2048
NOC = 1024
NPAT = 64
N_SCAN = 8


def draw_positions(key, part):
    first_key, second_key = jax.random.split(jax.random.fold_in(key, 11), 2)
    slot_ids = jnp.arange(NPAT, dtype=jnp.int32)
    band_start = slot_ids // SLOTS * TR
    row_offsets = band_start + jax.random.randint(first_key, (NPAT,), 0, TR, dtype=jnp.int32)
    row_offsets = jnp.minimum(row_offsets, NOR - W)
    row_offsets = row_offsets.at[0].set(0).at[NPAT - 1].set(NOR - W)
    col_offsets = jax.random.randint(second_key, (NPAT,), 0, NOC - W + 1, dtype=jnp.int32)
    col_offsets = col_offsets.at[0].set(0).at[1].set(NOC - W)
    return jnp.stack([row_offsets, col_offsets], axis=1).astype(jnp.int32)


def draw_counts(key, part):
    first_key, second_key, third_key = jax.random.split(jax.random.fold_in(key, 23), 3)
    values = jax.random.randint(first_key, (N_SCAN,), 1, SLOTS + 1, dtype=jnp.int32)
    full_index = jax.random.randint(second_key, (), 0, N_SCAN, dtype=jnp.int32)
    single_index = (full_index + 1 + jax.random.randint(third_key, (), 0, N_SCAN - 1, dtype=jnp.int32)) % N_SCAN
    values = values.at[full_index].set(SLOTS).at[single_index].set(1)
    return values.astype(jnp.int32)


def block_levels(rng, extent, cuts, smallest, top_value):
    level = 1.0
    for dim, blocks in cuts:
        steps = jax.random.uniform(jax.random.fold_in(jax.random.fold_in(rng, 6), dim), (blocks,), jnp.float32, smallest / len(cuts), top_value / len(cuts))
        level = level * jnp.repeat(jnp.exp(steps), extent[dim] // blocks).reshape((-1,) + (1,) * (len(extent) - 1 - dim))
    return level


def normal_values(stream_key, dims, spread, limit, pieces=(), kind=jnp.bfloat16):
    loudness = block_levels(stream_key, dims, pieces, -0.22, 0.18) if pieces else 1.0
    entries = jax.random.normal(stream_key, dims, jnp.float32) * spread * loudness
    return jnp.minimum(jnp.maximum(entries, -limit), limit).astype(kind)


def setup_inputs(seed: int = 0) -> dict:
    key_list = jax.random.split(jax.random.key(seed), 6)
    object_field = normal_values(key_list[0], (2, NOR, NOC), 0.7, 4.2, ((1, 8), (2, 4)), jnp.float32)
    probe_modes = normal_values(key_list[1], (MODES, 2, W, W), 0.35, 2.1, ((0, 4),), jnp.float32)
    amplitudes = jnp.clip(0.25 + 2.75 * jax.random.uniform(key_list[2], (NPAT, W, W), jnp.float32) ** block_levels(key_list[2], (NPAT, W, W), ((0, 8),), -0.2, 0.2), 0.25, 3.0).astype(jnp.bfloat16)
    positions = draw_positions(jax.random.fold_in(key_list[5], 71), 0)
    counts = draw_counts(jax.random.fold_in(key_list[5], 71), 0)
    return dict(object_field=object_field, probe_modes=probe_modes, amplitudes=amplitudes, positions=positions, counts=counts)


damping = 1.0
amp_floor = 0.5

def dft_tables(win_width):
    index_row = jnp.arange(win_width, dtype=jnp.int32)
    products = index_row[:, None] * index_row[None, :] % win_width
    phase_angle = products.astype(jnp.float32) * (2.0 * math.pi / win_width)
    norm_scale = 1.0 / math.sqrt(win_width)
    real_part = (jnp.cos(phase_angle) * norm_scale).astype(jnp.bfloat16)
    imag_part = (-jnp.sin(phase_angle) * norm_scale).astype(jnp.bfloat16)
    return (real_part, imag_part)

def transform(rowform, right_table, left_table, win_width):
    half_done = jnp.einsum('...ak,kl->...al', rowform.astype(jnp.float32), right_table.astype(jnp.float32), precision=lax.Precision.HIGHEST).astype(jnp.bfloat16)
    full_block = jnp.einsum('ca,...ak->...ck', left_table.astype(jnp.float32), half_done.astype(jnp.float32), precision=lax.Precision.HIGHEST)
    real_out = full_block[..., :win_width, :win_width] - full_block[..., win_width:, win_width:]
    imag_out = full_block[..., :win_width, win_width:] + full_block[..., win_width:, :win_width]
    return (real_out, imag_out)

def reference(object_field, probe_modes, amplitudes, positions, counts):
    real_part, imag_part = dft_tables(W)
    right_fwd = jnp.block([[real_part, imag_part], [-imag_part, real_part]])
    left_fwd = jnp.concatenate([real_part, imag_part], axis=0)
    right_inv = jnp.block([[real_part, -imag_part], [imag_part, real_part]])
    left_inv = jnp.concatenate([real_part, -imag_part], axis=0)
    object_low = object_field.astype(jnp.bfloat16)
    probe_re = probe_modes[:, 0]
    probe_im = probe_modes[:, 1]
    probe_power = lax.optimization_barrier(jnp.sum(probe_re * probe_re + probe_im * probe_im, axis=0))
    zero_index = jnp.zeros((), jnp.int32)

    def accumulate(running, inputs):
        buffer, grad_sum, weight_sum = running
        slot_index, place, amplitude = inputs
        row_at = place[0]
        col_at = place[1]
        window = lax.dynamic_slice(object_low, (zero_index, row_at, col_at), (2, W, W))
        live = (slot_index % SLOTS < counts[slot_index // SLOTS]).astype(jnp.float32)
        window_re = window[0].astype(jnp.float32)
        window_im = window[1].astype(jnp.float32)
        exit_wave = jnp.concatenate([probe_re * window_re - probe_im * window_im, probe_re * window_im + probe_im * window_re], axis=-1).astype(jnp.bfloat16)
        far_re, far_im = transform(exit_wave, right_fwd, left_fwd, W)
        intensity = lax.optimization_barrier(jnp.sum(far_re * far_re + far_im * far_im, axis=0))
        factor = live * (amplitude.astype(jnp.float32) / jnp.maximum(jnp.sqrt(intensity), amp_floor) - 1.0)
        change = jnp.concatenate([factor * far_re, factor * far_im], axis=-1).astype(jnp.bfloat16)
        near_re, near_im = transform(change, right_inv, left_inv, W)
        numer = jnp.stack([lax.optimization_barrier(jnp.sum(probe_re * near_re + probe_im * near_im, axis=0)), lax.optimization_barrier(jnp.sum(probe_re * near_im - probe_im * near_re, axis=0)), live * probe_power])
        grads = jnp.stack([window_re * near_re + window_im * near_im, window_re * near_im - window_im * near_re], axis=1)
        weight = window_re * window_re + window_im * window_im
        region = lax.dynamic_slice(buffer, (zero_index, row_at, col_at), (3, W, W))
        buffer = lax.dynamic_update_slice(buffer, region + numer, (zero_index, row_at, col_at))
        return ((buffer, grad_sum + grads, weight_sum + live * weight), None)
    init = (jnp.zeros((3, NOR, NOC), jnp.float32), jnp.zeros((MODES, 2, W, W), jnp.float32), jnp.zeros((W, W), jnp.float32))
    slot_ids = jnp.arange(NPAT, dtype=jnp.int32)
    (buffer, grad_sum, weight_sum), _ = lax.scan(accumulate, init, (slot_ids, positions, amplitudes))
    new_object = object_field + buffer[0:2] / (buffer[2] + damping)[None]
    probe_step = grad_sum / (weight_sum + damping)[None, None]
    return (new_object, probe_step)
```

```python
import math

import jax
import jax.numpy as jnp
import numpy as np
from jax import lax
from jax.experimental import pallas as pl
from jax.experimental.pallas import tpu as pltpu
from jax.sharding import PartitionSpec as P


damping = 1.0
amp_floor = 0.5
f32 = jnp.float32
bf16 = jnp.bfloat16


def shifted(value, axis, steps):
    count = lax.axis_size(axis)
    pairs = [(i, i + steps) for i in range(max(0, -steps), min(count, count - steps))]
    return lax.ppermute(value, axis, pairs)


def rotated(value, axis, steps):
    count = lax.axis_size(axis)
    return lax.ppermute(value, axis, [(i, (i + steps) % count) for i in range(count)])


def swapped(value, axis, mask):
    pairs = [(i, i ^ mask) for i in range(lax.axis_size(axis))]
    return lax.ppermute(value, axis, pairs)


def dft_tables(width):
    index = np.arange(width, dtype=np.int32)
    angle = (index[:, None] * index[None, :] % width).astype(np.float32) * np.float32(
        2.0 * math.pi / width
    )
    scale = np.float32(1.0 / math.sqrt(width))
    real = jnp.asarray(np.cos(angle) * scale, bf16)
    imag = jnp.asarray(-np.sin(angle) * scale, bf16)
    plus = jnp.block([[real, imag], [-imag, real]])
    minus = jnp.block([[real, -imag], [imag, real]])
    return plus, minus


def dot(a, b):
    return jnp.dot(a, b, preferred_element_type=f32)


def add_window(ref, lead, value, row, col, col_limit):
    width = value.shape[0]
    row_at = pl.multiple_of(row // 8 * 8, 8)
    col_at = pl.multiple_of(jnp.minimum(col // 128 * 128, col_limit - width - 128), 128)
    value = jnp.concatenate([value, jnp.zeros((8, width), f32)], 0)
    value = pltpu.roll(value, row - row_at, 0)
    value = jnp.concatenate([value, jnp.zeros((width + 8, 128), f32)], 1)
    value = pltpu.roll(value, col - col_at, 1)
    if lead is None:
        ref[pl.ds(row_at, width + 8), pl.ds(col_at, width + 128)] += value
    else:
        ref[lead, pl.ds(row_at, width + 8), pl.ds(col_at, width + 128)] += value


def cut_window(ref, lead, row, col, width, col_limit):
    row_at = pl.multiple_of(row // 16 * 16, 16)
    col_at = pl.multiple_of(jnp.minimum(col // 128 * 128, col_limit - width - 128), 128)
    value = ref[lead, pl.ds(row_at, width + 16), pl.ds(col_at, width + 128)].astype(f32)
    value = pltpu.roll(value, width + 128 - (col - col_at), 1)[:, :width]
    return pltpu.roll(value, width + 16 - (row - row_at), 0)[:width]


def main_kernel(tiles, slots, modes, width, band, spread, part):
    cols = tiles * band

    def body(*refs):
        meta = refs[0]
        blocks = refs[1 : 1 + tiles]
        rims = refs[1 + tiles : 1 + 2 * tiles]
        (
            own_probe,
            first_a,
            first_b,
            second_a,
            second_b,
            amp_ref,
            plus_ref,
            minus_ref,
            main_out,
            rim_out,
            power_out,
            *rest,
        ) = refs[1 + 2 * tiles :]
        odd_out = rest[0]
        even_out = rest[1]
        band_ref, probe, far, half, buffer, grads, win, fac, num, weight = rest[2:]
        scan_at = meta[0]
        tile_at = meta[1]
        local = modes // tiles
        for d in range(tiles):
            source = (tile_at - d + tiles) % tiles
            at = pl.multiple_of(source * band, band)
            for ch in range(2):
                band_ref[ch, 0:band, pl.ds(at, band)] = blocks[d][ch]
                band_ref[ch, band : 2 * band, pl.ds(at, band)] = rims[d][ch]
        for m in range(local):
            probe[tile_at * local + m] = own_probe[m]
        for k in range(spread // 2):
            for start, masks, pair in (
                (0, (2, 4), (first_a, first_b)),
                (local // 2, (4, 2), (second_a, second_b)),
            ):
                offset = (k & 1) * masks[0] + (k >> 1) * masks[1]
                for flip in range(2):
                    at = pl.multiple_of(((scan_at % spread) ^ (offset + flip)) * part, part)
                    for d in range(1, tiles):
                        source = (tile_at - d + tiles) % tiles
                        for m in range(local // 2):
                            for ch in range(2):
                                probe[source * local + start + m, ch, pl.ds(at, part), :] = pair[
                                    flip
                                ][k, d - 1, m, ch]
        power = jnp.zeros((width, width), f32)
        for m in range(modes):
            power = power + probe[m, 0] * probe[m, 0] + probe[m, 1] * probe[m, 1]
        power_out[...] = power
        buffer[...] = jnp.zeros_like(buffer)
        grads[...] = jnp.zeros_like(grads)
        weight[...] = jnp.zeros_like(weight)

        def one_slot(k, carry):
            slot = tile_at + tiles * k
            row = meta[2 + 2 * slot] - scan_at * band
            col = meta[3 + 2 * slot]
            live = (slot < meta[2 + 2 * slots * tiles]).astype(f32)
            for ch in range(2):
                win[ch] = cut_window(band_ref, ch, row, col, width, cols)
            weight[...] += live * (win[0] * win[0] + win[1] * win[1])
            fac[...] = jnp.zeros_like(fac)
            for m in range(modes):
                er = (probe[m, 0] * win[0] - probe[m, 1] * win[1]).astype(bf16)
                ei = (probe[m, 0] * win[1] + probe[m, 1] * win[0]).astype(bf16)
                h = dot(jnp.concatenate([er, ei], 1), plus_ref[...])
                half[m % 2, 0:width] = h[:, :width].astype(bf16)
                half[m % 2, width : 2 * width] = h[:, width:].astype(bf16)
                z = dot(minus_ref[...], half[m % 2])
                far[m] = z
                fac[...] += z[:width] * z[:width] + z[width:] * z[width:]
            fac[...] = live * (
                amp_ref[slot].astype(f32) / jnp.maximum(jnp.sqrt(fac[...]), amp_floor) - 1.0
            )
            num[...] = jnp.zeros_like(num)
            for m in range(modes):
                cr = (fac[...] * far[m, :width]).astype(bf16)
                ci = (fac[...] * far[m, width:]).astype(bf16)
                h = dot(jnp.concatenate([cr, ci], 1), minus_ref[...])
                half[m % 2, 0:width] = h[:, :width].astype(bf16)
                half[m % 2, width : 2 * width] = h[:, width:].astype(bf16)
                z = dot(plus_ref[...], half[m % 2])
                nr = z[:width]
                ni = z[width:]
                num[0] += probe[m, 0] * nr + probe[m, 1] * ni
                num[1] += probe[m, 0] * ni - probe[m, 1] * nr
                grads[2 * m] += win[0] * nr + win[1] * ni
                grads[2 * m + 1] += win[0] * ni - win[1] * nr
            for ch in range(2):
                add_window(buffer, ch, num[ch], row, col, cols)
            return carry

        lax.fori_loop(0, slots, one_slot, 0)
        for d in range(tiles):
            for ch in range(2):
                at = pl.multiple_of((tile_at + d) % tiles * band, band)
                main_out[d, ch] = buffer[ch, 0:band, pl.ds(at, band)].astype(bf16)
                rim_out[d, ch] = buffer[ch, band : 2 * band, pl.ds(at, band)].astype(bf16)
        for k in range(spread):
            at = pl.multiple_of(((scan_at % spread) ^ k) * part, part)
            out = odd_out if k % 2 else even_out
            for d in range(tiles):
                first = (tile_at + d) % tiles * local * 2
                for ch in range(2 * local):
                    value = grads[first + ch, pl.ds(at, part)]
                    out[k // 2, d * 2 * local + ch] = value.astype(out.dtype)
            out[k // 2, 2 * modes] = weight[pl.ds(at, part)].astype(out.dtype)

    return body


def illum_kernel(count, width, band):
    def body(meta, above, power, out, buffer):
        buffer[...] = jnp.zeros_like(buffer)
        corner_row = width - meta[0] * band
        corner_col = width - meta[1] * band

        def one(k, carry):
            mine = k < count
            slot = jnp.where(mine, k, k - count)
            live = slot < jnp.where(mine, meta[2 + 2 * count], above[2 * count])
            row = jnp.where(mine, meta[2 + 2 * slot], above[2 * slot]) + corner_row
            col = jnp.where(mine, meta[3 + 2 * slot], above[2 * slot + 1]) + corner_col

            @pl.when(live & (col > 0) & (col < width + band))
            def _():
                add_window(buffer, None, power[...], row, col, 2 * width + band)

            return carry

        lax.fori_loop(0, 2 * count, one, 0)
        out[...] = buffer[width : width + band, width : width + band]

    return body


def join_kernel(local, spread, part):
    def body(meta, steps, mates, out):
        for k in range(spread):
            at = pl.multiple_of(((meta[0] % spread) ^ k) * part, part)
            for m in range(local):
                for ch in range(2):
                    pick = mates if k % 2 else steps
                    out[m, ch, pl.ds(at, part), :] = pick[k // 2, 2 * m + ch]

    return body


def update(object_field, probe_modes, amplitudes, positions, counts):
    scans = lax.axis_size("scan")
    tiles = lax.axis_size("tile")
    scan_at = lax.axis_index("scan")
    tile_at = lax.axis_index("tile")
    slot_count, width = amplitudes.shape[:2]
    local = probe_modes.shape[0]
    modes = local * tiles
    band = object_field.shape[1]
    slots = slot_count // tiles
    spread = min(scans, 8)
    part = width // spread
    ids = jnp.stack([scan_at, tile_at]).astype(jnp.int32)
    spots = jnp.concatenate([positions.reshape(-1), counts])
    meta = jnp.concatenate([ids, spots])
    above = shifted(spots, "scan", 1)

    piece = lax.dynamic_slice_in_dim(probe_modes, (scan_at % spread) * part, part, 2)
    pieces = jnp.stack([rotated(piece, "tile", d) for d in range(1, tiles)])[None]
    first = pieces[:, :, : local // 2]
    second = pieces[:, :, local // 2 :]
    first = jnp.concatenate([first, swapped(first, "scan", 2)])
    second = jnp.concatenate([second, swapped(second, "scan", 4)])
    first = jnp.concatenate([first, swapped(first, "scan", 4)])
    second = jnp.concatenate([second, swapped(second, "scan", 2)])
    first_mate = swapped(first, "scan", 1)
    second_mate = swapped(second, "scan", 1)

    low = object_field.astype(bf16)
    blocks = [low] + [rotated(low, "tile", d) for d in range(1, tiles)]
    rims = [shifted(b, "scan", -1) for b in blocks]

    plus, minus = dft_tables(width)
    vmem = pl.BlockSpec(memory_space=pltpu.VMEM)
    smem = pl.BlockSpec(memory_space=pltpu.SMEM)
    main, rim, power, odd, even = pl.pallas_call(
        main_kernel(tiles, slots, modes, width, band, spread, part),
        out_shape=(
            jax.ShapeDtypeStruct((tiles, 2, band, band), bf16),
            jax.ShapeDtypeStruct((tiles, 2, band, band), bf16),
            jax.ShapeDtypeStruct((width, width), f32),
            jax.ShapeDtypeStruct((spread // 2, 2 * modes + 1, part, width), bf16),
            jax.ShapeDtypeStruct((spread // 2, 2 * modes + 1, part, width), f32),
        ),
        in_specs=[smem] + [vmem] * (2 * tiles + 8),
        out_specs=(vmem,) * 5,
        scratch_shapes=[
            pltpu.VMEM((2, 2 * band, tiles * band), bf16),
            pltpu.VMEM((modes, 2, width, width), f32),
            pltpu.VMEM((modes, 2 * width, width), f32),
            pltpu.VMEM((2, 2 * width, width), bf16),
            pltpu.VMEM((2, 2 * band, tiles * band), f32),
            pltpu.VMEM((2 * modes, width, width), f32),
            pltpu.VMEM((2, width, width), f32),
            pltpu.VMEM((width, width), f32),
            pltpu.VMEM((2, width, width), f32),
            pltpu.VMEM((width, width), f32),
        ],
        name="update",
    )(
        meta,
        *blocks,
        *rims,
        probe_modes,
        first,
        first_mate,
        second,
        second_mate,
        amplitudes,
        plus,
        minus,
    )

    share = main.astype(f32) + shifted(rim, "scan", 1).astype(f32)
    totals = share[0]
    for d in range(1, tiles):
        totals = totals + rotated(share[d].astype(bf16), "tile", d).astype(f32)

    illumination = pl.pallas_call(
        illum_kernel(slot_count, width, band),
        out_shape=jax.ShapeDtypeStruct((band, band), f32),
        in_specs=[smem] * 2 + [vmem],
        out_specs=vmem,
        scratch_shapes=[pltpu.VMEM((2 * width + band, 2 * width + band), f32)],
        name="illumination",
    )(meta, above, power)
    new_object = object_field + totals / (illumination + damping)

    even = even + swapped(odd, "scan", 1).astype(f32)
    total = even[0]
    for k in range(1, spread // 2):
        total = total + swapped(even[k].astype(bf16), "scan", 2 * k).astype(f32)
    mask = spread
    while mask < scans:
        total = total + swapped(total, "scan", mask)
        mask *= 2
    step = None
    for d in range(tiles):
        share = jnp.concatenate([total[2 * local * d : 2 * local * (d + 1)], total[2 * modes :]])
        share = rotated(share, "tile", d) if d else share
        step = share if step is None else step + share
    step = step[: 2 * local] / (step[2 * local] + damping)
    steps = [step] + [swapped(step, "scan", 2 * k) for k in range(1, spread // 2)]
    steps = jnp.stack(steps)
    mates = swapped(steps, "scan", 1)
    probe_step = pl.pallas_call(
        join_kernel(local, spread, part),
        out_shape=jax.ShapeDtypeStruct(probe_modes.shape, f32),
        in_specs=[smem, vmem, vmem],
        out_specs=vmem,
        name="join",
    )(meta, steps, mates)
    return (new_object, probe_step)


def solution(mesh):
    placed = (
        P(None, "scan", "tile"),
        P("tile", None, None, None),
        P("scan", None, None),
        P("scan", None),
        P("scan"),
    )
    return jax.shard_map(
        update,
        mesh=mesh,
        in_specs=placed,
        out_specs=(P(None, "scan", "tile"), P("tile", None, None, None)),
        check_vma=False,
    )
```

```python
import math

import jax
import jax.numpy as jnp
import numpy as np
from jax import lax
from jax.experimental import pallas as pl
from jax.experimental.pallas import tpu as pltpu
from jax.sharding import PartitionSpec as P


damping = 1.0
amp_floor = 0.5
f32 = jnp.float32
bf16 = jnp.bfloat16


def shifted(value, axis, steps):
    count = lax.axis_size(axis)
    pairs = [(i, i + steps) for i in range(max(0, -steps), min(count, count - steps))]
    return lax.ppermute(value, axis, pairs)


def rotated(value, axis, steps):
    count = lax.axis_size(axis)
    return lax.ppermute(value, axis, [(i, (i + steps) % count) for i in range(count)])


def swapped(value, axis, mask):
    pairs = [(i, i ^ mask) for i in range(lax.axis_size(axis))]
    return lax.ppermute(value, axis, pairs)


def dft_tables(width):
    index = np.arange(width, dtype=np.int32)
    angle = (index[:, None] * index[None, :] % width).astype(np.float32) * np.float32(
        2.0 * math.pi / width
    )
    scale = np.float32(1.0 / math.sqrt(width))
    real = jnp.asarray(np.cos(angle) * scale, bf16)
    imag = jnp.asarray(-np.sin(angle) * scale, bf16)
    plus = jnp.block([[real, imag], [-imag, real]])
    minus = jnp.block([[real, -imag], [imag, real]])
    return plus, minus


def dot(a, b):
    return jnp.dot(a, b, preferred_element_type=f32)


def add_window(ref, lead, value, row, col, col_limit):
    width = value.shape[0]
    row_at = pl.multiple_of(row // 8 * 8, 8)
    col_at = pl.multiple_of(jnp.minimum(col // 128 * 128, col_limit - width - 128), 128)
    value = jnp.concatenate([value, jnp.zeros((8, width), f32)], 0)
    value = pltpu.roll(value, row - row_at, 0)
    value = jnp.concatenate([value, jnp.zeros((width + 8, 128), f32)], 1)
    value = pltpu.roll(value, col - col_at, 1)
    if lead is None:
        ref[pl.ds(row_at, width + 8), pl.ds(col_at, width + 128)] += value
    else:
        ref[lead, pl.ds(row_at, width + 8), pl.ds(col_at, width + 128)] += value


def cut_window(ref, lead, row, col, width, col_limit):
    row_at = pl.multiple_of(row // 16 * 16, 16)
    col_at = pl.multiple_of(jnp.minimum(col // 128 * 128, col_limit - width - 128), 128)
    value = ref[lead, pl.ds(row_at, width + 16), pl.ds(col_at, width + 128)].astype(f32)
    value = pltpu.roll(value, width + 128 - (col - col_at), 1)[:, :width]
    return pltpu.roll(value, width + 16 - (row - row_at), 0)[:width]


def main_kernel(tiles, slots, modes, width, band, spread, part):
    cols = tiles * band

    def body(*refs):
        meta = refs[0]
        blocks = refs[1 : 1 + tiles]
        rims = refs[1 + tiles : 1 + 2 * tiles]
        (
            own_probe,
            first_a,
            first_b,
            second_a,
            second_b,
            amp_ref,
            plus_ref,
            minus_ref,
            main_out,
            rim_out,
            power_out,
            *rest,
        ) = refs[1 + 2 * tiles :]
        odd_out = rest[0]
        even_out = rest[1]
        band_ref, probe, far, half, buffer, grads, win, fac, num, weight = rest[2:]
        scan_at = meta[0]
        tile_at = meta[1]
        local = modes // tiles
        for d in range(tiles):
            source = (tile_at - d + tiles) % tiles
            at = pl.multiple_of(source * band, band)
            for ch in range(2):
                band_ref[ch, 0:band, pl.ds(at, band)] = blocks[d][ch]
                band_ref[ch, band : 2 * band, pl.ds(at, band)] = rims[d][ch]
        for m in range(local):
            probe[tile_at * local + m] = own_probe[m]
        for k in range(spread // 2):
            for start, masks, pair in (
                (0, (2, 4), (first_a, first_b)),
                (local // 2, (4, 2), (second_a, second_b)),
            ):
                offset = (k & 1) * masks[0] + (k >> 1) * masks[1]
                for flip in range(2):
                    at = pl.multiple_of(((scan_at % spread) ^ (offset + flip)) * part, part)
                    for d in range(1, tiles):
                        source = (tile_at - d + tiles) % tiles
                        for m in range(local // 2):
                            for ch in range(2):
                                probe[source * local + start + m, ch, pl.ds(at, part), :] = pair[
                                    flip
                                ][k, d - 1, m, ch]
        power = jnp.zeros((width, width), f32)
        for m in range(modes):
            power = power + probe[m, 0] * probe[m, 0] + probe[m, 1] * probe[m, 1]
        power_out[...] = power
        buffer[...] = jnp.zeros_like(buffer)
        grads[...] = jnp.zeros_like(grads)
        weight[...] = jnp.zeros_like(weight)

        def one_slot(k, carry):
            slot = tile_at + tiles * k
            row = meta[2 + 2 * slot] - scan_at * band
            col = meta[3 + 2 * slot]
            live = (slot < meta[2 + 2 * slots * tiles]).astype(f32)
            for ch in range(2):
                win[ch] = cut_window(band_ref, ch, row, col, width, cols)
            weight[...] += live * (win[0] * win[0] + win[1] * win[1])
            fac[...] = jnp.zeros_like(fac)
            for m in range(modes):
                er = (probe[m, 0] * win[0] - probe[m, 1] * win[1]).astype(bf16)
                ei = (probe[m, 0] * win[1] + probe[m, 1] * win[0]).astype(bf16)
                h = dot(jnp.concatenate([er, ei], 1), plus_ref[...])
                half[m % 2, 0:width] = h[:, :width].astype(bf16)
                half[m % 2, width : 2 * width] = h[:, width:].astype(bf16)
                z = dot(minus_ref[...], half[m % 2])
                far[m] = z
                fac[...] += z[:width] * z[:width] + z[width:] * z[width:]
            fac[...] = live * (
                amp_ref[slot].astype(f32) / jnp.maximum(jnp.sqrt(fac[...]), amp_floor) - 1.0
            )
            num[...] = jnp.zeros_like(num)
            for m in range(modes):
                cr = (fac[...] * far[m, :width]).astype(bf16)
                ci = (fac[...] * far[m, width:]).astype(bf16)
                h = dot(jnp.concatenate([cr, ci], 1), minus_ref[...])
                half[m % 2, 0:width] = h[:, :width].astype(bf16)
                half[m % 2, width : 2 * width] = h[:, width:].astype(bf16)
                z = dot(plus_ref[...], half[m % 2])
                nr = z[:width]
                ni = z[width:]
                num[0] += probe[m, 0] * nr + probe[m, 1] * ni
                num[1] += probe[m, 0] * ni - probe[m, 1] * nr
                grads[2 * m] += win[0] * nr + win[1] * ni
                grads[2 * m + 1] += win[0] * ni - win[1] * nr
            for ch in range(2):
                add_window(buffer, ch, num[ch], row, col, cols)
            return carry

        lax.fori_loop(0, slots, one_slot, 0)
        for d in range(tiles):
            for ch in range(2):
                at = pl.multiple_of((tile_at + d) % tiles * band, band)
                main_out[d, ch] = buffer[ch, 0:band, pl.ds(at, band)].astype(bf16)
                rim_out[d, ch] = buffer[ch, band : 2 * band, pl.ds(at, band)].astype(bf16)
        for k in range(spread):
            at = pl.multiple_of(((scan_at % spread) ^ k) * part, part)
            out = odd_out if k % 2 else even_out
            for d in range(tiles):
                first = (tile_at + d) % tiles * local * 2
                for ch in range(2 * local):
                    value = grads[first + ch, pl.ds(at, part)]
                    out[k // 2, d * 2 * local + ch] = value.astype(out.dtype)
            out[k // 2, 2 * modes] = weight[pl.ds(at, part)].astype(out.dtype)

    return body


def illum_kernel(count, width, band):
    def body(meta, above, power, out, buffer):
        buffer[...] = jnp.zeros_like(buffer)
        corner_row = width - meta[0] * band
        corner_col = width - meta[1] * band

        def one(k, carry):
            mine = k < count
            slot = jnp.where(mine, k, k - count)
            live = slot < jnp.where(mine, meta[2 + 2 * count], above[2 * count])
            row = jnp.where(mine, meta[2 + 2 * slot], above[2 * slot]) + corner_row
            col = jnp.where(mine, meta[3 + 2 * slot], above[2 * slot + 1]) + corner_col

            @pl.when(live & (col > 0) & (col < width + band))
            def _():
                add_window(buffer, None, power[...], row, col, 2 * width + band)

            return carry

        lax.fori_loop(0, 2 * count, one, 0)
        out[...] = buffer[width : width + band, width : width + band]

    return body


def join_kernel(local, spread, part):
    def body(meta, *refs):
        out = refs[spread]
        for k in range(spread):
            at = pl.multiple_of(((meta[0] % spread) ^ k) * part, part)
            for m in range(local):
                for ch in range(2):
                    pick = refs[k // 2 + k % 2 * (spread // 2)]
                    out[m, ch, pl.ds(at, part), :] = pick[2 * m + ch]

    return body


def update(object_field, probe_modes, amplitudes, positions, counts):
    scans = lax.axis_size("scan")
    tiles = lax.axis_size("tile")
    scan_at = lax.axis_index("scan")
    tile_at = lax.axis_index("tile")
    slot_count, width = amplitudes.shape[:2]
    local = probe_modes.shape[0]
    modes = local * tiles
    band = object_field.shape[1]
    slots = slot_count // tiles
    spread = min(scans, 8)
    part = width // spread
    ids = jnp.stack([scan_at, tile_at]).astype(jnp.int32)
    spots = jnp.concatenate([positions.reshape(-1), counts])
    meta = jnp.concatenate([ids, spots])
    above = shifted(spots, "scan", 1)

    piece = lax.dynamic_slice_in_dim(probe_modes, (scan_at % spread) * part, part, 2)
    pieces = jnp.stack([rotated(piece, "tile", d) for d in range(1, tiles)])[None]
    first = pieces[:, :, : local // 2]
    second = pieces[:, :, local // 2 :]
    first = jnp.concatenate([first, swapped(first, "scan", 2)])
    second = jnp.concatenate([second, swapped(second, "scan", 4)])
    first = jnp.concatenate([first, swapped(first, "scan", 4)])
    second = jnp.concatenate([second, swapped(second, "scan", 2)])
    first_mate = swapped(first, "scan", 1)
    second_mate = swapped(second, "scan", 1)

    low = object_field.astype(bf16)
    blocks = [low] + [rotated(low, "tile", d) for d in range(1, tiles)]
    rims = [shifted(b, "scan", -1) for b in blocks]

    plus, minus = dft_tables(width)
    vmem = pl.BlockSpec(memory_space=pltpu.VMEM)
    smem = pl.BlockSpec(memory_space=pltpu.SMEM)
    main, rim, power, odd, even = pl.pallas_call(
        main_kernel(tiles, slots, modes, width, band, spread, part),
        out_shape=(
            jax.ShapeDtypeStruct((tiles, 2, band, band), bf16),
            jax.ShapeDtypeStruct((tiles, 2, band, band), bf16),
            jax.ShapeDtypeStruct((width, width), f32),
            jax.ShapeDtypeStruct((spread // 2, 2 * modes + 1, part, width), bf16),
            jax.ShapeDtypeStruct((spread // 2, 2 * modes + 1, part, width), f32),
        ),
        in_specs=[smem] + [vmem] * (2 * tiles + 8),
        out_specs=(vmem,) * 5,
        scratch_shapes=[
            pltpu.VMEM((2, 2 * band, tiles * band), bf16),
            pltpu.VMEM((modes, 2, width, width), f32),
            pltpu.VMEM((modes, 2 * width, width), f32),
            pltpu.VMEM((2, 2 * width, width), bf16),
            pltpu.VMEM((2, 2 * band, tiles * band), f32),
            pltpu.VMEM((2 * modes, width, width), f32),
            pltpu.VMEM((2, width, width), f32),
            pltpu.VMEM((width, width), f32),
            pltpu.VMEM((2, width, width), f32),
            pltpu.VMEM((width, width), f32),
        ],
        name="update",
    )(
        meta,
        *blocks,
        *rims,
        probe_modes,
        first,
        first_mate,
        second,
        second_mate,
        amplitudes,
        plus,
        minus,
    )

    share = main.astype(f32) + shifted(rim, "scan", 1).astype(f32)
    totals = share[0]
    for d in range(1, tiles):
        totals = totals + rotated(share[d].astype(bf16), "tile", d).astype(f32)

    illumination = pl.pallas_call(
        illum_kernel(slot_count, width, band),
        out_shape=jax.ShapeDtypeStruct((band, band), f32),
        in_specs=[smem] * 2 + [vmem],
        out_specs=vmem,
        scratch_shapes=[pltpu.VMEM((2 * width + band, 2 * width + band), f32)],
        name="illumination",
    )(meta, above, power)
    new_object = object_field + totals / (illumination + damping)

    even = even + swapped(odd, "scan", 1).astype(f32)
    total = even[0]
    for k in range(1, spread // 2):
        total = total + swapped(even[k].astype(bf16), "scan", 2 * k).astype(f32)
    mask = spread
    while mask < scans:
        total = total + swapped(total, "scan", mask)
        mask *= 2
    step = None
    for d in range(tiles):
        share = jnp.concatenate([total[2 * local * d : 2 * local * (d + 1)], total[2 * modes :]])
        share = rotated(share.astype(bf16), "tile", d).astype(f32) if d else share
        step = share if step is None else step + share
    step = step[: 2 * local] / (step[2 * local] + damping)
    steps = [step] + [swapped(step, "scan", 2 * k) for k in range(1, spread // 2)]
    steps += [swapped(value, "scan", 1) for value in steps]
    probe_step = pl.pallas_call(
        join_kernel(local, spread, part),
        out_shape=jax.ShapeDtypeStruct(probe_modes.shape, f32),
        in_specs=[smem] + [vmem] * spread,
        out_specs=vmem,
        name="join",
    )(meta, *steps)
    return (new_object, probe_step)


def solution(mesh):
    placed = (
        P(None, "scan", "tile"),
        P("tile", None, None, None),
        P("scan", None, None),
        P("scan", None),
        P("scan"),
    )
    return jax.shard_map(
        update,
        mesh=mesh,
        in_specs=placed,
        out_specs=(P(None, "scan", "tile"), P("tile", None, None, None)),
        check_vma=False,
    )
```

```python
import math

import jax
import jax.numpy as jnp
import numpy as np
from jax import lax
from jax.experimental import pallas as pl
from jax.experimental.pallas import tpu as pltpu
from jax.sharding import PartitionSpec as P


damping = 1.0
amp_floor = 0.5
f32 = jnp.float32
bf16 = jnp.bfloat16


def shifted(value, axis, steps):
    count = lax.axis_size(axis)
    pairs = [(i, i + steps) for i in range(max(0, -steps), min(count, count - steps))]
    return lax.ppermute(value, axis, pairs)


def rotated(value, axis, steps):
    count = lax.axis_size(axis)
    return lax.ppermute(value, axis, [(i, (i + steps) % count) for i in range(count)])


def swapped(value, axis, mask):
    pairs = [(i, i ^ mask) for i in range(lax.axis_size(axis))]
    return lax.ppermute(value, axis, pairs)


def dft_tables(width):
    index = np.arange(width, dtype=np.int32)
    angle = (index[:, None] * index[None, :] % width).astype(np.float32) * np.float32(
        2.0 * math.pi / width
    )
    scale = np.float32(1.0 / math.sqrt(width))
    real = jnp.asarray(np.cos(angle) * scale, bf16)
    imag = jnp.asarray(-np.sin(angle) * scale, bf16)
    plus = jnp.block([[real, imag], [-imag, real]])
    minus = jnp.block([[real, -imag], [imag, real]])
    return plus, minus


def dot(a, b):
    return jnp.dot(a, b, preferred_element_type=f32)


def add_window(ref, lead, value, row, col, col_limit):
    width = value.shape[0]
    row_at = pl.multiple_of(row // 8 * 8, 8)
    col_at = pl.multiple_of(jnp.minimum(col // 128 * 128, col_limit - width - 128), 128)
    value = jnp.concatenate([value, jnp.zeros((8, width), f32)], 0)
    value = pltpu.roll(value, row - row_at, 0)
    value = jnp.concatenate([value, jnp.zeros((width + 8, 128), f32)], 1)
    value = pltpu.roll(value, col - col_at, 1)
    if lead is None:
        ref[pl.ds(row_at, width + 8), pl.ds(col_at, width + 128)] += value
    else:
        ref[lead, pl.ds(row_at, width + 8), pl.ds(col_at, width + 128)] += value


def cut_window(ref, lead, row, col, width, col_limit):
    row_at = pl.multiple_of(row // 16 * 16, 16)
    col_at = pl.multiple_of(jnp.minimum(col // 128 * 128, col_limit - width - 128), 128)
    value = ref[lead, pl.ds(row_at, width + 16), pl.ds(col_at, width + 128)].astype(f32)
    value = pltpu.roll(value, width + 128 - (col - col_at), 1)[:, :width]
    return pltpu.roll(value, width + 16 - (row - row_at), 0)[:width]


def main_kernel(tiles, slots, modes, width, band, spread, part):
    cols = tiles * band

    def body(*refs):
        meta = refs[0]
        blocks = refs[1 : 1 + tiles]
        rims = refs[1 + tiles : 1 + 2 * tiles]
        (
            own_probe,
            first_a,
            first_b,
            second_a,
            second_b,
            amp_ref,
            plus_ref,
            minus_ref,
            main_out,
            rim_out,
            power_out,
            *rest,
        ) = refs[1 + 2 * tiles :]
        odd_out = rest[0]
        even_out = rest[1]
        band_ref, probe, far, half, buffer, grads, win, fac, num, weight = rest[2:]
        scan_at = meta[0]
        tile_at = meta[1]
        local = modes // tiles
        for d in range(tiles):
            source = (tile_at - d + tiles) % tiles
            at = pl.multiple_of(source * band, band)
            for ch in range(2):
                band_ref[ch, 0:band, pl.ds(at, band)] = blocks[d][ch]
                band_ref[ch, band : 2 * band, pl.ds(at, band)] = rims[d][ch]
        for m in range(local):
            probe[tile_at * local + m] = own_probe[m]
        for k in range(spread // 2):
            for start, masks, pair in (
                (0, (2, 4), (first_a, first_b)),
                (local // 2, (4, 2), (second_a, second_b)),
            ):
                offset = (k & 1) * masks[0] + (k >> 1) * masks[1]
                for flip in range(2):
                    at = pl.multiple_of(((scan_at % spread) ^ (offset + flip)) * part, part)
                    for d in range(1, tiles):
                        source = (tile_at - d + tiles) % tiles
                        for m in range(local // 2):
                            for ch in range(2):
                                probe[source * local + start + m, ch, pl.ds(at, part), :] = pair[
                                    flip
                                ][k, d - 1, m, ch]
        power = jnp.zeros((width, width), f32)
        for m in range(modes):
            power = power + probe[m, 0] * probe[m, 0] + probe[m, 1] * probe[m, 1]
        power_out[...] = power
        buffer[...] = jnp.zeros_like(buffer)
        grads[...] = jnp.zeros_like(grads)
        weight[...] = jnp.zeros_like(weight)

        def one_slot(k, carry):
            slot = tile_at + tiles * k
            row = meta[2 + 2 * slot] - scan_at * band
            col = meta[3 + 2 * slot]
            live = (slot < meta[2 + 2 * slots * tiles]).astype(f32)
            for ch in range(2):
                win[ch] = cut_window(band_ref, ch, row, col, width, cols)
            weight[...] += live * (win[0] * win[0] + win[1] * win[1])
            fac[...] = jnp.zeros_like(fac)
            for m in range(modes):
                er = (probe[m, 0] * win[0] - probe[m, 1] * win[1]).astype(bf16)
                ei = (probe[m, 0] * win[1] + probe[m, 1] * win[0]).astype(bf16)
                h = dot(jnp.concatenate([er, ei], 1), plus_ref[...])
                half[m % 2, 0:width] = h[:, :width].astype(bf16)
                half[m % 2, width : 2 * width] = h[:, width:].astype(bf16)
                z = dot(minus_ref[...], half[m % 2])
                far[m] = z
                fac[...] += z[:width] * z[:width] + z[width:] * z[width:]
            fac[...] = live * (
                amp_ref[slot].astype(f32) / jnp.maximum(jnp.sqrt(fac[...]), amp_floor) - 1.0
            )
            num[...] = jnp.zeros_like(num)
            for m in range(modes):
                cr = (fac[...] * far[m, :width]).astype(bf16)
                ci = (fac[...] * far[m, width:]).astype(bf16)
                h = dot(jnp.concatenate([cr, ci], 1), minus_ref[...])
                half[m % 2, 0:width] = h[:, :width].astype(bf16)
                half[m % 2, width : 2 * width] = h[:, width:].astype(bf16)
                z = dot(plus_ref[...], half[m % 2])
                nr = z[:width]
                ni = z[width:]
                num[0] += probe[m, 0] * nr + probe[m, 1] * ni
                num[1] += probe[m, 0] * ni - probe[m, 1] * nr
                grads[2 * m] += win[0] * nr + win[1] * ni
                grads[2 * m + 1] += win[0] * ni - win[1] * nr
            below = lax.broadcasted_iota(jnp.int32, (width, width), 0) < row + width - band
            for ch in range(2):
                add_window(buffer, ch, num[ch], row, col, cols)
                rim_out[k, ch] = jnp.where(
                    below, pltpu.roll(num[ch], row + width - band, 0), 0.0
                ).astype(bf16)
            return carry

        lax.fori_loop(0, slots, one_slot, 0)
        for ch in range(2):
            main_out[ch] = buffer[ch, 0:band].astype(bf16)
        for k in range(spread):
            at = pl.multiple_of(((scan_at % spread) ^ k) * part, part)
            out = odd_out if k % 2 else even_out
            for d in range(tiles):
                first = (tile_at + d) % tiles * local * 2
                for ch in range(2 * local):
                    value = grads[first + ch, pl.ds(at, part)]
                    out[k // 2, d * 2 * local + ch] = value.astype(out.dtype)
            out[k // 2, 2 * modes] = weight[pl.ds(at, part)].astype(out.dtype)

    return body


def rim_kernel(tiles, slots, width, band):
    cols = tiles * band

    def body(meta, above, main, lower, *rest):
        outs, buffer = rest[:tiles], rest[tiles]
        buffer[...] = main[...].astype(f32)
        for k in range(slots):
            col = above[2 * (meta[1] + tiles * k) + 1]
            col_at = pl.multiple_of(jnp.minimum(col // 128 * 128, cols - width - 128), 128)
            for ch in range(2):
                value = lower[k, ch].astype(f32)
                value = jnp.concatenate([value, jnp.zeros((width, 128), f32)], 1)
                buffer[ch, 0:width, pl.ds(col_at, width + 128)] += pltpu.roll(
                    value, col - col_at, 1
                )
        for d in range(tiles):
            at = pl.multiple_of((meta[1] + d) % tiles * band, band)
            for ch in range(2):
                outs[d][ch] = buffer[ch, :, pl.ds(at, band)].astype(outs[d].dtype)

    return body


def illum_kernel(count, width, band):
    def body(meta, above, power, out, buffer):
        buffer[...] = jnp.zeros_like(buffer)
        corner_row = width - meta[0] * band
        corner_col = width - meta[1] * band

        def one(k, carry):
            mine = k < count
            slot = jnp.where(mine, k, k - count)
            live = slot < jnp.where(mine, meta[2 + 2 * count], above[2 * count])
            row = jnp.where(mine, meta[2 + 2 * slot], above[2 * slot]) + corner_row
            col = jnp.where(mine, meta[3 + 2 * slot], above[2 * slot + 1]) + corner_col

            @pl.when(live & (col > 0) & (col < width + band))
            def _():
                add_window(buffer, None, power[...], row, col, 2 * width + band)

            return carry

        lax.fori_loop(0, 2 * count, one, 0)
        out[...] = buffer[width : width + band, width : width + band]

    return body


def join_kernel(local, spread, part):
    def body(meta, *refs):
        out = refs[spread]
        for k in range(spread):
            at = pl.multiple_of(((meta[0] % spread) ^ k) * part, part)
            for m in range(local):
                for ch in range(2):
                    pick = refs[k // 2 + k % 2 * (spread // 2)]
                    out[m, ch, pl.ds(at, part), :] = pick[2 * m + ch]

    return body


def update(object_field, probe_modes, amplitudes, positions, counts):
    scans = lax.axis_size("scan")
    tiles = lax.axis_size("tile")
    scan_at = lax.axis_index("scan")
    tile_at = lax.axis_index("tile")
    slot_count, width = amplitudes.shape[:2]
    local = probe_modes.shape[0]
    modes = local * tiles
    band = object_field.shape[1]
    slots = slot_count // tiles
    spread = min(scans, 8)
    part = width // spread
    ids = jnp.stack([scan_at, tile_at]).astype(jnp.int32)
    spots = jnp.concatenate([positions.reshape(-1), counts])
    meta = jnp.concatenate([ids, spots])
    above = shifted(spots, "scan", 1)

    piece = lax.dynamic_slice_in_dim(probe_modes, (scan_at % spread) * part, part, 2)
    pieces = jnp.stack([rotated(piece, "tile", d) for d in range(1, tiles)])[None]
    first = pieces[:, :, : local // 2]
    second = pieces[:, :, local // 2 :]
    first = jnp.concatenate([first, swapped(first, "scan", 2)])
    second = jnp.concatenate([second, swapped(second, "scan", 4)])
    first = jnp.concatenate([first, swapped(first, "scan", 4)])
    second = jnp.concatenate([second, swapped(second, "scan", 2)])
    first_mate = swapped(first, "scan", 1)
    second_mate = swapped(second, "scan", 1)

    low = object_field.astype(bf16)
    blocks = [low] + [rotated(low, "tile", d) for d in range(1, tiles)]
    rims = [shifted(b, "scan", -1) for b in blocks]

    plus, minus = dft_tables(width)
    vmem = pl.BlockSpec(memory_space=pltpu.VMEM)
    smem = pl.BlockSpec(memory_space=pltpu.SMEM)
    main, rim, power, odd, even = pl.pallas_call(
        main_kernel(tiles, slots, modes, width, band, spread, part),
        out_shape=(
            jax.ShapeDtypeStruct((2, band, tiles * band), bf16),
            jax.ShapeDtypeStruct((slots, 2, width, width), bf16),
            jax.ShapeDtypeStruct((width, width), f32),
            jax.ShapeDtypeStruct((spread // 2, 2 * modes + 1, part, width), bf16),
            jax.ShapeDtypeStruct((spread // 2, 2 * modes + 1, part, width), f32),
        ),
        in_specs=[smem] + [vmem] * (2 * tiles + 8),
        out_specs=(vmem,) * 5,
        scratch_shapes=[
            pltpu.VMEM((2, 2 * band, tiles * band), bf16),
            pltpu.VMEM((modes, 2, width, width), f32),
            pltpu.VMEM((modes, 2 * width, width), f32),
            pltpu.VMEM((2, 2 * width, width), bf16),
            pltpu.VMEM((2, 2 * band, tiles * band), f32),
            pltpu.VMEM((2 * modes, width, width), f32),
            pltpu.VMEM((2, width, width), f32),
            pltpu.VMEM((width, width), f32),
            pltpu.VMEM((2, width, width), f32),
            pltpu.VMEM((width, width), f32),
        ],
        name="update",
    )(
        meta,
        *blocks,
        *rims,
        probe_modes,
        first,
        first_mate,
        second,
        second_mate,
        amplitudes,
        plus,
        minus,
    )

    lower = shifted(rim, "scan", 1)
    kept, *sent = pl.pallas_call(
        rim_kernel(tiles, slots, width, band),
        out_shape=(jax.ShapeDtypeStruct((2, band, band), f32),)
        + (jax.ShapeDtypeStruct((2, band, band), bf16),) * (tiles - 1),
        in_specs=[smem, smem, vmem, vmem],
        out_specs=(vmem,) * tiles,
        scratch_shapes=[pltpu.VMEM((2, band, tiles * band), f32)],
        name="rims",
    )(meta, above, main, lower)
    totals = kept
    for d in range(1, tiles):
        totals = totals + rotated(sent[d - 1], "tile", d).astype(f32)

    illumination = pl.pallas_call(
        illum_kernel(slot_count, width, band),
        out_shape=jax.ShapeDtypeStruct((band, band), f32),
        in_specs=[smem] * 2 + [vmem],
        out_specs=vmem,
        scratch_shapes=[pltpu.VMEM((2 * width + band, 2 * width + band), f32)],
        name="illumination",
    )(meta, above, power)
    new_object = object_field + totals / (illumination + damping)

    even = even + swapped(odd, "scan", 1).astype(f32)
    total = even[0]
    for k in range(1, spread // 2):
        total = total + swapped(even[k].astype(bf16), "scan", 2 * k).astype(f32)
    mask = spread
    while mask < scans:
        total = total + swapped(total, "scan", mask)
        mask *= 2
    step = None
    for d in range(tiles):
        share = jnp.concatenate([total[2 * local * d : 2 * local * (d + 1)], total[2 * modes :]])
        share = rotated(share.astype(bf16), "tile", d).astype(f32) if d else share
        step = share if step is None else step + share
    step = step[: 2 * local] / (step[2 * local] + damping)
    steps = [step] + [swapped(step, "scan", 2 * k) for k in range(1, spread // 2)]
    steps += [swapped(value, "scan", 1) for value in steps]
    probe_step = pl.pallas_call(
        join_kernel(local, spread, part),
        out_shape=jax.ShapeDtypeStruct(probe_modes.shape, f32),
        in_specs=[smem] + [vmem] * spread,
        out_specs=vmem,
        name="join",
    )(meta, *steps)
    return (new_object, probe_step)


def solution(mesh):
    placed = (
        P(None, "scan", "tile"),
        P("tile", None, None, None),
        P("scan", None, None),
        P("scan", None),
        P("scan"),
    )
    return jax.shard_map(
        update,
        mesh=mesh,
        in_specs=placed,
        out_specs=(P(None, "scan", "tile"), P("tile", None, None, None)),
        check_vma=False,
    )
```
